1024 devices in a mesh: grp: 4 (over y_lo), slab: 8 (over x), brick: 32 (over z, y_hi, core).
Axes of the slice: x: 8, y: 8 (y_hi: 2, y_lo: 4; y = y_hi * 4 + y_lo), z: 8, core: 2. Of those that a mesh axis runs over, the one named last changes fastest.
Arguments:
- voxel_warmth: float32 [128, 64, 8192], P('slab', 'grp', 'brick'), may hold values from -6 to 6
- consolidated_flag: int32 [128, 64, 8192], P('slab', 'grp', 'brick'), may hold values 0 or 1
- beam_north_position: int32 [2, 4], replicated, may hold values from 0 to 63
- beam_east_position: int32 [2, 4], replicated, may hold values from 0 to 8191
Outputs:
- warmth_after_substep: float32 [128, 64, 8192], P('slab', 'grp', 'brick')
- coarse_shift_vector: float32 [3, 64, 32, 4096], P(None, 'slab', 'grp', 'brick')
The draws below stay inside these ranges and needn't reach their ends.
All inputs are finite; a program needn't handle non-finite values. No bound on the sum of `consolidated_flag` on one device may be relied on, other than what follows from the above.
Results may differ from the reference program's by a relative error of at most 0.0001.
Values sent between devices are 32-bit elements; how exact they have to be, the bound alone decides.
A program may use at most 64 MiB of HBM per device.

```python
import jax
import jax.numpy as jnp
from jax import lax

SUBSTEPS = 2
SWEEPS = 6
SPOTS = 4
BRICKS_UPWARD = 128
BRICKS_ACROSS_N = 64
BRICKS_ACROSS_E = 8192


def with_ends(values, stream_key, low, largest):
    index_at = [jax.random.randint(jax.random.fold_in(stream_key, axis), (), 0, length) for axis, length in enumerate(values.shape)]
    longest = values.shape.index(max(values.shape))
    next_to = index_at[:longest] + [(index_at[longest] + 1) % values.shape[longest]] + index_at[longest + 1:]
    return values.at[tuple(index_at)].set(low).at[tuple(next_to)].set(largest)


def block_scale(stream_key, dims, cuts, low, largest):
    factor_of, own = 1.0, jax.random.fold_in(stream_key, 6)
    for position, parts in cuts:
        heights = jnp.exp(jax.random.uniform(jax.random.fold_in(own, position), (parts,), jnp.float32, low / len(cuts), largest / len(cuts)))
        factor_of = factor_of * jnp.repeat(heights, dims[position] // parts).reshape([-1 if axis == position else 1 for axis in range(len(dims))])
    return factor_of


def centred(stream_key, dims, width, reach, cuts=(), held_as=jnp.bfloat16):
    drawn = width * jax.random.normal(stream_key, dims, jnp.float32)
    if cuts:
        drawn = drawn * block_scale(stream_key, dims, cuts, -0.22, 0.18)
    return jnp.clip(drawn, -reach, reach).astype(held_as)


def setup_inputs(seed: int = 0) -> dict:
    streams_of = jax.random.split(jax.random.key(seed), 5)
    return {
        "voxel_warmth": centred(streams_of[0], (BRICKS_UPWARD, BRICKS_ACROSS_N, BRICKS_ACROSS_E), 1.0, 6.0, ((0, 8), (1, 4), (2, 32)), jnp.float32),
        "consolidated_flag": with_ends((jax.random.randint(streams_of[1], (BRICKS_UPWARD, BRICKS_ACROSS_N, BRICKS_ACROSS_E), 0, 3) < 2).astype(jnp.int32), jax.random.fold_in(streams_of[1], 1), 0, 1),
        "beam_north_position": with_ends(jax.random.randint(streams_of[2], (SUBSTEPS, SPOTS), 0, BRICKS_ACROSS_N), jax.random.fold_in(streams_of[2], 1), 0, BRICKS_ACROSS_N - 1).astype(jnp.int32),
        "beam_east_position": with_ends(jax.random.randint(streams_of[3], (SUBSTEPS, SPOTS), 0, BRICKS_ACROSS_E), jax.random.fold_in(streams_of[3], 1), 0, BRICKS_ACROSS_E - 1).astype(jnp.int32),
    }


time_step = 0.15
spot_power = 30.0
solid_kappa = 1.0
powder_kappa = 0.2
shear_modulus = 1.0
coupling = 1.5
stress_factor = 8.0
eigen_low = 0.5
eigen_high = 3.5


def neighbour(padded, axis_pick, forward):
    pieces = []
    for axis_number in range(3):
        if axis_number == axis_pick:
            pieces.append(slice(2, None) if forward else slice(0, -2))
        else:
            pieces.append(slice(1, -1))
    return padded[tuple(pieces)]


def thermal_advance(bordered_warmth, bordered_diffusivity, injected_power):
    centre_heat = bordered_warmth[1:-1, 1:-1, 1:-1]
    centre_kappa = bordered_diffusivity[1:-1, 1:-1, 1:-1]
    total = jnp.zeros_like(centre_heat)
    for axis_pick in range(3):
        for forward in (True, False):
            other_kappa = neighbour(bordered_diffusivity, axis_pick, forward)
            other_heat = neighbour(bordered_warmth, axis_pick, forward)
            face = 2.0 * centre_kappa * other_kappa / (centre_kappa + other_kappa)
            total = total + face * (other_heat - centre_heat)
    capacity = 0.375 + 0.625 * centre_kappa
    return centre_heat + time_step * (total + injected_power) / capacity


def laser_source(row_y, row_x, start_z, start_y, start_x, shape_zyx, top_layer):
    vertical_span, count_across_north, count_across_east = shape_zyx
    zpos = start_z + jnp.arange(vertical_span, dtype=jnp.int32)
    ypos = start_y + jnp.arange(count_across_north, dtype=jnp.int32)
    xpos = start_x + jnp.arange(count_across_east, dtype=jnp.int32)
    hit_rows = (ypos[None, :] == row_y[:, None]).astype(jnp.float32)
    hit_columns = (xpos[None, :] == row_x[:, None]).astype(jnp.float32)
    plane = jnp.dot(hit_rows.T, hit_columns, precision=lax.Precision.HIGHEST, preferred_element_type=jnp.float32)
    layer = (zpos == top_layer - 1).astype(jnp.float32)
    return spot_power * layer[:, None, None] * plane[None, :, :]


def kappa_from(consolidated_flag):
    return powder_kappa + (solid_kappa - powder_kappa) * consolidated_flag.astype(jnp.float32)


def merge_blocks(field):
    vertical_span, count_across_north, count_across_east = field.shape
    blocks = field.reshape(vertical_span // 2, 2, count_across_north // 2, 2, count_across_east // 2, 2)
    return jnp.sum(blocks, axis=(1, 3, 5)) * 0.125


def thermal_force(padded):
    half = 0.5 * stress_factor
    return jnp.stack([
        half * (padded[:-2, 1:-1, 1:-1] - padded[2:, 1:-1, 1:-1]),
        half * (padded[1:-1, :-2, 1:-1] - padded[1:-1, 2:, 1:-1]),
        half * (padded[1:-1, 1:-1, :-2] - padded[1:-1, 1:-1, 2:]),
    ])


def apply_operator(padded, spring):
    centre = padded[:, 1:-1, 1:-1, 1:-1]
    neighbours = (padded[:, 2:, 1:-1, 1:-1] + padded[:, :-2, 1:-1, 1:-1]
                  + padded[:, 1:-1, 2:, 1:-1] + padded[:, 1:-1, :-2, 1:-1]
                  + padded[:, 1:-1, 1:-1, 2:] + padded[:, 1:-1, 1:-1, :-2])
    divergence = ((padded[0, 1:, :-1, :-1] - padded[0, :-1, :-1, :-1])
                  + (padded[1, :-1, 1:, :-1] - padded[1, :-1, :-1, :-1])
                  + (padded[2, :-1, :-1, 1:] - padded[2, :-1, :-1, :-1]))
    inner = divergence[1:, 1:, 1:]
    backward = jnp.stack([
        divergence[:-1, 1:, 1:] - inner,
        divergence[1:, :-1, 1:] - inner,
        divergence[1:, 1:, :-1] - inner,
    ])
    return shear_modulus * (6.0 * centre - neighbours) + coupling * backward + spring * centre


def reference(voxel_warmth, consolidated_flag, beam_north_position, beam_east_position):
    kappa = kappa_from(consolidated_flag)
    bordered_diffusivity = jnp.pad(kappa, 1)
    warmth_after_substep = voxel_warmth
    for substep in range(SUBSTEPS):
        injected_power = laser_source(beam_north_position[substep], beam_east_position[substep], 0, 0, 0, (BRICKS_UPWARD, BRICKS_ACROSS_N, BRICKS_ACROSS_E), BRICKS_UPWARD)
        warmth_after_substep = thermal_advance(jnp.pad(warmth_after_substep, 1), bordered_diffusivity, injected_power)
    dense_material_flag = consolidated_flag.astype(jnp.float32)
    deformation_gradient = merge_blocks(dense_material_flag * warmth_after_substep)
    spring = 0.5 + 1.5 * merge_blocks(dense_material_flag)
    force = thermal_force(jnp.pad(deformation_gradient, 1))
    diagonal = 6.0 * shear_modulus + 2.0 * coupling + spring
    centre_value = (eigen_high + eigen_low) / 2.0
    radius = (eigen_high - eigen_low) / 2.0
    sigma_ratio = centre_value / radius
    rho_prev = 1.0 / sigma_ratio
    coarse_shift_vector = jnp.zeros_like(force)
    residual = force
    direction = (residual / diagonal) * (1.0 / centre_value)
    for sweep_index in range(SWEEPS):
        coarse_shift_vector = coarse_shift_vector + direction
        if sweep_index + 1 < SWEEPS:
            padded = jnp.pad(direction, ((0, 0), (1, 1), (1, 1), (1, 1)))
            residual = residual - apply_operator(padded, spring)
            rho_next = 1.0 / (2.0 * sigma_ratio - rho_prev)
            direction = (rho_next * rho_prev) * direction + (2.0 * rho_next / radius) * (residual / diagonal)
            rho_prev = rho_next
    return warmth_after_substep, coarse_shift_vector
```

```python
import functools

import jax
import jax.numpy as jnp
from jax import lax
from jax.experimental import pallas as pl
from jax.experimental.pallas import tpu as pltpu
from jax.sharding import PartitionSpec as P

SWEEPS = 6
time_step = 0.15
spot_power = 30.0
shear_modulus = 1.0
coupling = 1.5
stress_factor = 8.0
eigen_low = 0.5
eigen_high = 3.5

MESH = pl.DeviceIdType.MESH
OUTSIDE = -4.0

DIRS = [(1, 0), (-1, 0), (0, 1), (0, -1), (1, 1), (1, -1), (-1, 1), (-1, -1)]

f32 = jnp.float32
bf16 = jnp.bfloat16


def lanes(n):
    return lax.broadcasted_iota(jnp.int32, (8, n), 1)


def conductance(s):
    return jnp.maximum(jnp.maximum(s * (2.0 / 15.0) + 0.2, s * (2.0 / 3.0) - (1.0 / 3.0)), 0.0)


def conductances(e_ref, g_ref):
    planes, rows, width = e_ref.shape[1:]

    def body(z, _):
        f = e_ref[0, z]
        up = e_ref[0, jnp.minimum(z + 1, planes - 1)]
        g_ref[0, z] = conductance(f + pltpu.roll(f, width - 1, 1))
        g_ref[1, z] = conductance(f + pltpu.roll(f, rows - 1, 0))
        g_ref[2, z] = conductance(f + up)
        g_ref[3, z] = (2.0 * time_step) - time_step * f
        return 0

    lax.fori_loop(0, planes, body, 0)


def thermal(t_in, t_out, g_ref, source, first, last):
    rows, width = g_ref.shape[2:]

    def body(z, _):
        t = t_in[z]
        fx = g_ref[0, z] * (pltpu.roll(t, width - 1, 1) - t)
        fy = g_ref[1, z] * (pltpu.roll(t, rows - 1, 0) - t)
        fz = g_ref[2, z] * (t_in[z + 1] - t)
        fb = g_ref[2, z - 1] * (t - t_in[z - 1])
        total = (fx - pltpu.roll(fx, 1, 1)) + (fy - pltpu.roll(fy, 1, 0)) + (fz - fb)
        t_out[z] = t + g_ref[3, z] * total
        return 0

    lax.fori_loop(first, last, body, 0)
    t_out[17] = t_out[17] + g_ref[3, 17] * source


def laser(by_ref, bx_ref, substep, ypos, xpos, scale):
    total = jnp.zeros(ypos.shape, f32)
    for p in range(4):
        hit = (ypos == by_ref[substep, p]) & (xpos == bx_ref[substep, p])
        total = total + jnp.where(hit, scale, 0.0)
    return total


def kernel(w_hbm, f_hbm, by_ref, bx_ref, t_out, u_out,
           w_v, f_v, em, ew, gm, gw, t1m, t1w, t2m, t2w,
           zs, zr, ys, yr, ds, dr, xs, xr, qs, cb, czr, cyr, cdr,
           cx, dira, dirb, res, inv, spr, div, pick, t_v,
           load_sem, send_sem, recv_sem, out_sem):
    me = {a: lax.axis_index(a) for a in ("slab", "grp", "brick")}
    size = {a: lax.axis_size(a) for a in ("slab", "grp", "brick")}

    def has(off):
        found = None
        for a, d in zip(("slab", "grp", "brick"), off):
            if d:
                one = me[a] < size[a] - 1 if d > 0 else me[a] > 0
                found = one if found is None else found & one
        return found

    def device(off):
        return {a: me[a] + d for a, d in zip(("slab", "grp", "brick"), off)}

    def negative(off):
        return tuple(-d for d in off)

    neighbours = [d + (0,) for d in DIRS] + [(0, 0, 1), (0, 0, -1)]

    barrier = pltpu.get_barrier_semaphore()
    count = jnp.int32(0)
    for off in neighbours:
        @pl.when(has(off))
        def _(off=off):
            pl.semaphore_signal(barrier, inc=1, device_id=device(off), device_id_type=MESH)
        count = count + has(off).astype(jnp.int32)

    load_w = pltpu.make_async_copy(w_hbm, w_v, load_sem.at[0])
    load_f = pltpu.make_async_copy(f_hbm, f_v, load_sem.at[1])
    load_w.start()
    load_f.start()

    k = lax.broadcasted_iota(jnp.int32, (384, 256), 0)
    c = lax.broadcasted_iota(jnp.int32, (384, 256), 1)
    h = c - 128
    base = jnp.where(c < 128, 2 * c, jnp.where(h < 64, 256 + 32 + 2 * h, 256 + 2 * h - 160))
    used = (c < 128) | (h < 8) | (h >= 120)
    pick[...] = jnp.where(used & ((k == base) | (k == base + 1)), 1.0, 0.0).astype(bf16)

    on_top = jnp.where(me["slab"] == size["slab"] - 1, spot_power, 0.0).astype(f32)
    y0 = me["grp"] * 16 - 4
    x0 = me["brick"] * 256
    ym = lax.broadcasted_iota(jnp.int32, (24, 256), 0) + y0
    xm = lax.broadcasted_iota(jnp.int32, (24, 256), 1) + x0
    yw = lax.broadcasted_iota(jnp.int32, (24, 128), 0) + y0
    lw = lax.broadcasted_iota(jnp.int32, (24, 128), 1)
    xw = jnp.where(lw < 64, lw + 224, lw - 96) + x0

    em[:, 0:2] = jnp.zeros((2, 2, 24, 256), f32)
    em[:, 18:20] = jnp.zeros((2, 2, 24, 256), f32)

    load_f.wait()
    load_w.wait()
    edge = jnp.zeros((16, 4, 256), f32)
    em[0, 2:18] = jnp.concatenate([edge, f_v[...].astype(f32), edge], axis=1)
    em[1, 2:18] = jnp.concatenate([edge, w_v[...], edge], axis=1)
    for i, z in ((0, 14), (1, 0)):
        zs[i, 0] = f_v[z : z + 2].astype(f32)
        zs[i, 1] = w_v[z : z + 2]
        ys[i, 0] = f_v[:, z : z + 2, :].astype(f32)
        ys[i, 1] = w_v[:, z : z + 2, :]
    for i, (dz, dy) in enumerate(DIRS[4:]):
        z, y = (15 if dz > 0 else 0), (15 if dy > 0 else 0)
        ds[i, 0:1] = f_v[z, y : y + 1, :].astype(f32)
        ds[i, 1:2] = w_v[z, y : y + 1, :]

    pl.semaphore_wait(barrier, count)

    def copy(source, target, slot, off):
        return pltpu.make_async_remote_copy(
            src_ref=source, dst_ref=target, send_sem=send_sem.at[slot], recv_sem=recv_sem.at[slot],
            device_id=device(off), device_id_type=MESH)

    def start(messages):
        for source, target, slot, off, fill in messages:
            @pl.when(has(off))
            def _(source=source, target=target, slot=slot, off=off):
                copy(source, target, slot, off).start()

    def receive(messages):
        for source, target, slot, off, fill in messages:
            there = has(negative(off))

            @pl.when(there)
            def _(source=source, target=target, slot=slot, off=off):
                copy(source, target, slot, off).wait_recv()

            @pl.when(jnp.logical_not(there))
            def _(target=target, fill=fill):
                fill(target)

    def sent(messages):
        for source, target, slot, off, fill in messages:
            @pl.when(has(off))
            def _(source=source, target=target, slot=slot, off=off):
                copy(source, target, slot, off).wait_send()

    def fill_pair(target):
        shape = target.shape[1:]
        target[0] = jnp.full(shape, OUTSIDE, f32)
        target[1] = jnp.zeros(shape, f32)

    def fill_row(target):
        row = lax.broadcasted_iota(jnp.int32, (2, 256), 0)
        target[...] = jnp.where(row == 0, OUTSIDE, 0.0).astype(f32)

    raw = []
    for slot, d in enumerate(DIRS):
        off = d + (0,)
        if slot < 2:
            raw.append((zs.at[slot], zr.at[slot], slot, off, fill_pair))
        elif slot < 4:
            raw.append((ys.at[slot - 2], yr.at[slot - 2], slot, off, fill_pair))
        else:
            raw.append((ds.at[slot - 4], dr.at[slot - 4], slot, off, fill_row))
    start(raw)
    receive(raw)

    em[:, 0:2, 4:20, :] = zr[0]
    em[:, 18:20, 4:20, :] = zr[1]
    em[:, 2:18, 2:4, :] = yr[0]
    em[:, 2:18, 20:22, :] = yr[1]
    for i, (dz, dy) in enumerate(DIRS[4:]):
        z, y = (1 if dz > 0 else 18), (3 if dy > 0 else 20)
        for f in range(2):
            em[f, z, y : y + 1, :] = dr[i, f : f + 1, :]

    slot_of = lanes(128) // 16
    for f in range(2):
        for v in range(8):
            right, left = jnp.zeros((8, 128), f32), jnp.zeros((8, 128), f32)
            for j in range(8):
                r = 8 * v + j
                if r < 60:
                    z, y = r // 3, 8 * (r % 3)
                    right = jnp.where(slot_of == j, pltpu.roll(em[f, z, y : y + 8, 128:256], (16 * j - 112) % 128, 1), right)
                    left = jnp.where(slot_of == j, pltpu.roll(em[f, z, y : y + 8, 0:128], 16 * j, 1) if j else em[f, z, y : y + 8, 0:128], left)
            xs[0, f, v] = right
            xs[1, f, v] = left
    along = [(xs.at[i], xr.at[i], 8 + i, (0, 0, 1 - 2 * i), fill_pair) for i in range(2)]
    start(along)

    conductances(em, gm)
    thermal(em.at[1], t1m, gm, laser(by_ref, bx_ref, 0, ym, xm, on_top), 1, 19)
    thermal(t1m, t2m, gm, laser(by_ref, bx_ref, 1, ym, xm, on_top), 2, 18)

    receive(along)
    lane = lanes(128)
    for f in range(2):
        for r in range(60):
            v, j = r // 8, r % 8
            z, y = r // 3, 8 * (r % 3)
            own = jnp.where(lane < 64, pltpu.roll(em[f, z, y : y + 8, 128:256], 32, 1), pltpu.roll(em[f, z, y : y + 8, 0:128], 96, 1))
            before, after = xr[0, f, v], xr[1, f, v]
            before = pltpu.roll(before, (80 - 16 * j) % 128, 1) if (80 - 16 * j) % 128 else before
            after = pltpu.roll(after, (32 - 16 * j) % 128, 1) if (32 - 16 * j) % 128 else after
            own = jnp.where((lane >= 32) & (lane < 48), after, own)
            ew[f, z, y : y + 8, :] = jnp.where((lane >= 80) & (lane < 96), before, own)
    conductances(ew, gw)
    thermal(ew.at[1], t1w, gw, laser(by_ref, bx_ref, 0, yw, xw, on_top), 1, 19)
    thermal(t1w, t2w, gw, laser(by_ref, bx_ref, 1, yw, xw, on_top), 2, 18)

    lane16 = lax.broadcasted_iota(jnp.int32, (16, 128), 1)

    def merge(zp, _):
        sums = [None] * 6
        for d in range(2):
            z = 2 * zp + d
            w = t2w[z + 2, 4:20, :]
            a = jnp.where(lane16 < 16, pltpu.roll(w, 32, 1), t2m[z + 2, 4:20, 0:128])
            b = jnp.where(lane16 >= 112, pltpu.roll(w, 96, 1), t2m[z + 2, 4:20, 128:256])
            t_v[z, :, 0:128] = a
            t_v[z, :, 128:256] = b
            fa, fb, fw = em[0, z + 2, 4:20, 0:128], em[0, z + 2, 4:20, 128:256], ew[0, z + 2, 4:20, :]
            for i, piece in enumerate((fa * a, fb * b, fw * w, fa, fb, fw)):
                sums[i] = piece if sums[i] is None else sums[i] + piece
        for i in range(6):
            qs[i // 3, i % 3, zp] = sums[i]
        return 0

    lax.fori_loop(0, 8, merge, 0)
    save = pltpu.make_async_copy(t_v, t_out, out_sem.at[0])
    save.start()

    rows = []
    for f in range(2):
        tiles = [
            (qs[f, t, :, pl.ds(0, 8, stride=2), :] + qs[f, t, :, pl.ds(1, 8, stride=2), :]).reshape(64, 128)
            for t in range(3)
        ]
        rows.append(jnp.concatenate(tiles, axis=1) * 0.125)
    q, solid = rows
    q1 = q.astype(bf16)
    rest = q - q1.astype(f32)
    q2 = rest.astype(bf16)
    q3 = (rest - q2.astype(f32)).astype(bf16)
    coarse = jnp.dot(jnp.concatenate([q1, q2, q3, solid.astype(bf16)], axis=0), pick[...], preferred_element_type=f32)
    strain = (coarse[0:64] + coarse[64:128]) + coarse[128:192]
    fields = [strain.reshape(8, 8, 256), coarse[192:256].reshape(8, 8, 256)]
    for f in range(2):
        packed = jnp.zeros((8, 128), f32)
        for z in range(8):
            packed = jnp.where(slot_of == z, pltpu.roll(fields[f][z, :, 128:256], (8 + 16 * z) % 128, 1), packed)
            cb[f, 1 + z] = fields[f][z, :, 0:128]
            cx[f, 6 + z, 8:16, :] = fields[f][z]
        cb[f, 0] = packed
        cb[f, 9] = packed

    def fill_coarse(target):
        shape = target.shape[1:]
        target[0] = jnp.zeros(shape, f32)
        target[1] = jnp.full(shape, OUTSIDE, f32)

    last6, first6 = cb.at[:, 3:10], cb.at[:, 0:7]
    swap = []
    for slot, d in enumerate(DIRS):
        off = d + (0,)
        if slot < 2:
            source, target = (last6, first6)[slot], czr.at[slot]
        elif slot < 4:
            source, target = cb.at[:, 0:9], cyr.at[slot - 2]
        else:
            source, target = (last6 if d[0] > 0 else first6), cdr.at[slot - 4]
        swap.append((source, target, 10 + slot, off, fill_coarse))
    start(swap)
    receive(swap)

    rim = (lane < 8) | (lane >= 120)

    def place(block, f, first_plane, zs_, packed, tile):
        p = block[f, packed]
        for i, z in enumerate(zs_):
            at = first_plane[1] + i
            cx[f, at, 8 * tile : 8 * tile + 8, 0:128] = block[f, first_plane[0] + i]
            back = (-(8 + 16 * z)) % 128
            cx[f, at, 8 * tile : 8 * tile + 8, 128:256] = jnp.where(rim, pltpu.roll(p, back, 1) if back else p, 0.0)

    upper, lower = range(2, 8), range(0, 6)
    for f in range(2):
        place(czr.at[0], f, (0, 0), upper, 6, 1)
        place(czr.at[1], f, (1, 14), lower, 0, 1)
        place(cyr.at[0], f, (1, 6), range(8), 0, 0)
        place(cyr.at[1], f, (1, 6), range(8), 0, 2)
        for i, (dz, dy) in enumerate(DIRS[4:]):
            if dz > 0:
                place(cdr.at[i], f, (0, 0), upper, 6, 0 if dy > 0 else 2)
            else:
                place(cdr.at[i], f, (1, 14), lower, 0, 0 if dy > 0 else 2)

    sweeps(cx, u_out, dira, dirb, res, inv, spr, div)
    save.wait()
    sent(raw)
    sent(along)
    sent(swap)


def sweeps(cx, u_out, dira, dirb, res, inv, spr, div):
    centre_value = (eigen_high + eigen_low) / 2.0
    radius = (eigen_high - eigen_low) / 2.0
    sigma = centre_value / radius
    rho = 1.0 / sigma
    half = 0.5 * stress_factor
    next_x = lambda a: pltpu.roll(a, 255, 1)
    prev_x = lambda a: pltpu.roll(a, 1, 1)
    next_y = lambda a: pltpu.roll(a, 23, 0)
    prev_y = lambda a: pltpu.roll(a, 1, 0)

    def begin(z, _):
        solid = cx[1, z]
        spring = 0.5 + 1.5 * solid
        inverse = jnp.where(solid < -1.0, 0.0, 1.0 / (6.0 * shear_modulus + 2.0 * coupling + spring))
        inv[z] = inverse
        spr[z] = spring + 6.0 * shear_modulus
        s = cx[0, z]
        force = (half * (cx[0, z - 1] - cx[0, z + 1]), half * (prev_y(s) - next_y(s)), half * (prev_x(s) - next_x(s)))
        for d in range(3):
            res[d, z] = force[d]
            dira[d, z] = force[d] * inverse * (1.0 / centre_value)
        return 0

    lax.fori_loop(1, 19, begin, 0)
    for d in range(3):
        u_out[d] = dira[d, 6:14, 8:16, 0:128]

    old, new = dira, dirb
    for sweep in range(SWEEPS - 1):
        halo = SWEEPS - 2 - sweep
        rho_next = 1.0 / (2.0 * sigma - rho)
        keep, gain = rho_next * rho, 2.0 * rho_next / radius

        def spread(z, _, old=old):
            a, b, c = old[0, z], old[1, z], old[2, z]
            div[z] = (old[0, z + 1] - a) + (next_y(b) - b) + (next_x(c) - c)
            return 0

        lax.fori_loop(6 - halo - 1, 14 + halo, spread, 0)

        def step(z, _, old=old, new=new, keep=keep, gain=gain):
            here = div[z]
            back = (div[z - 1] - here, prev_y(here) - here, prev_x(here) - here)
            factor, inverse = spr[z], inv[z] * gain
            for d in range(3):
                v = old[d, z]
                around = (old[d, z + 1] + old[d, z - 1]) + (next_y(v) + prev_y(v)) + (next_x(v) + prev_x(v))
                r = res[d, z] - (factor * v - shear_modulus * around + coupling * back[d])
                res[d, z] = r
                new[d, z] = keep * v + inverse * r
            return 0

        lax.fori_loop(6 - halo, 14 + halo, step, 0)
        for d in range(3):
            u_out[d] = u_out[d] + new[d, 6:14, 8:16, 0:128]
        rho = rho_next
        old, new = new, old


def per_device(warmth, flag, north, east):
    vmem = pltpu.VMEM
    ext = lambda *s: vmem(s, f32)
    scratch = [
        ext(16, 16, 256), vmem((16, 16, 256), jnp.int32),
        ext(2, 20, 24, 256), ext(2, 20, 24, 128), ext(4, 20, 24, 256), ext(4, 20, 24, 128),
        ext(20, 24, 256), ext(20, 24, 128), ext(20, 24, 256), ext(20, 24, 128),
        ext(2, 2, 2, 16, 256), ext(2, 2, 2, 16, 256), ext(2, 2, 16, 2, 256), ext(2, 2, 16, 2, 256), ext(4, 2, 256), ext(4, 2, 256),
        ext(2, 2, 8, 8, 128), ext(2, 2, 8, 8, 128), ext(2, 3, 8, 16, 128),
        ext(2, 10, 8, 128), ext(2, 2, 7, 8, 128), ext(2, 2, 9, 8, 128), ext(4, 2, 7, 8, 128),
        ext(2, 20, 24, 256), ext(3, 20, 24, 256), ext(3, 20, 24, 256), ext(3, 20, 24, 256), ext(20, 24, 256), ext(20, 24, 256), ext(20, 24, 256),
        vmem((384, 256), bf16), ext(16, 16, 256),
        pltpu.SemaphoreType.DMA((2,)), pltpu.SemaphoreType.DMA((18,)), pltpu.SemaphoreType.DMA((18,)), pltpu.SemaphoreType.DMA((1,)),
    ]
    return pl.pallas_call(
        kernel,
        out_shape=(jax.ShapeDtypeStruct((16, 16, 256), f32), jax.ShapeDtypeStruct((3, 8, 8, 128), f32)),
        in_specs=[
            pl.BlockSpec(memory_space=pl.ANY),
            pl.BlockSpec(memory_space=pl.ANY),
            pl.BlockSpec(memory_space=pltpu.SMEM),
            pl.BlockSpec(memory_space=pltpu.SMEM),
        ],
        out_specs=(pl.BlockSpec(memory_space=pl.ANY), pl.BlockSpec(memory_space=pltpu.VMEM)),
        scratch_shapes=scratch,
        compiler_params=pltpu.CompilerParams(collective_id=0, has_side_effects=True),
    )(warmth, flag, north, east)


def solution(mesh):
    in_specs = (P("slab", "grp", "brick"), P("slab", "grp", "brick"), P(), P())
    out_specs = (P("slab", "grp", "brick"), P(None, "slab", "grp", "brick"))
    return jax.shard_map(per_device, mesh=mesh, in_specs=in_specs, out_specs=out_specs, check_vma=False)
```

```python
import functools

import jax
import jax.numpy as jnp
from jax import lax
from jax.experimental import pallas as pl
from jax.experimental.pallas import tpu as pltpu
from jax.sharding import PartitionSpec as P

SWEEPS = 6
time_step = 0.15
spot_power = 30.0
shear_modulus = 1.0
coupling = 1.5
stress_factor = 8.0
eigen_low = 0.5
eigen_high = 3.5

MESH = pl.DeviceIdType.MESH
OUTSIDE = -4.0

DIRS = [(1, 0), (-1, 0), (0, 1), (0, -1), (1, 1), (1, -1), (-1, 1), (-1, -1)]

f32 = jnp.float32
bf16 = jnp.bfloat16


def lane_of(rows):
    return lax.broadcasted_iota(jnp.int32, (rows, 128), 1)


def next_x(tiles):
    rolled = [pltpu.roll(t, 127, 1) for t in tiles]
    if len(tiles) == 1:
        return rolled
    end = lane_of(tiles[0].shape[0]) == 127
    return [jnp.where(end, rolled[1 - i], rolled[i]) for i in range(2)]


def prev_x(tiles):
    rolled = [pltpu.roll(t, 1, 1) for t in tiles]
    if len(tiles) == 1:
        return rolled
    end = lane_of(tiles[0].shape[0]) == 0
    return [jnp.where(end, rolled[1 - i], rolled[i]) for i in range(2)]


def conductance(s):
    return jnp.maximum(jnp.maximum(s * (2.0 / 15.0) + 0.2, s * (2.0 / 3.0) - (1.0 / 3.0)), 0.0)


def conductances(e, g, tiles):
    for z in range(19):
        f = [e[0, t, z, 2:26, :] for t in tiles]
        fx = next_x(f) if z else None
        for i, t in enumerate(tiles):
            g[2, t, z, 2:26, :] = conductance(f[i] + e[0, t, z + 1, 2:26, :])
            if z:
                g[0, t, z, 2:26, :] = conductance(f[i] + fx[i])
                g[1, t, z, 2:26, :] = conductance(f[i] + e[0, t, z, 3:27, :])
                g[3, t, z, 2:26, :] = (2.0 * time_step) - time_step * f[i]


def thermal(t_in, t_out, g, source, tiles, first, last, r, n):
    below = [g[2, t, first - 1, r : r + n, :] * (t_in(t, first, r) - t_in(t, first - 1, r)) for t in tiles]
    for z in range(first, last):
        here = [t_in(t, z, r) for t in tiles]
        ahead = next_x(here)
        fx = [g[0, t, z, r : r + n, :] * (ahead[i] - here[i]) for i, t in enumerate(tiles)]
        back = prev_x(fx)
        for i, t in enumerate(tiles):
            fy = g[1, t, z, r : r + n, :] * (t_in(t, z, r + 1) - here[i])
            by = g[1, t, z, r - 1 : r + n - 1, :] * (here[i] - t_in(t, z, r - 1))
            fz = g[2, t, z, r : r + n, :] * (t_in(t, z + 1, r) - here[i])
            total = (fx[i] - back[i]) + (fy - by) + (fz - below[i])
            if z == 17:
                total = total + source[i]
            t_out(t, z, here[i] + g[3, t, z, r : r + n, :] * total)
            below[i] = fz


def kernel(w_hbm, f_hbm, by_hbm, bx_hbm, t_out, u_out,
           w_v, f_v, by_ref, bx_ref, e, g, t1, t2,
           zs, zr, ys, yr, ds, dr, xs, xr, qs, cbm, cbw, czr, cyr, cdr, cwr,
           cx, dira, dirb, res, inv, spr, div, pick_m, pick_w, t_v, u_v,
           load_sem, send_sem, recv_sem, out_sem):
    me = {a: lax.axis_index(a) for a in ("slab", "grp", "brick")}
    size = {a: lax.axis_size(a) for a in ("slab", "grp", "brick")}

    def has(off):
        found = None
        for a, d in zip(("slab", "grp", "brick"), off):
            if d:
                one = me[a] < size[a] - 1 if d > 0 else me[a] > 0
                found = one if found is None else found & one
        return found

    def device(off):
        return {a: me[a] + d for a, d in zip(("slab", "grp", "brick"), off)}

    def negative(off):
        return tuple(-d for d in off)

    loads = [
        pltpu.make_async_copy(source, target, load_sem.at[i])
        for i, (source, target) in enumerate(((f_hbm, f_v), (w_hbm, w_v), (by_hbm, by_ref), (bx_hbm, bx_ref)))
    ]
    for load in loads:
        load.start()

    neighbours = [d + (0,) for d in DIRS] + [(0, 0, 1), (0, 0, -1)]
    barrier = pltpu.get_barrier_semaphore()
    count = jnp.int32(0)
    for off in neighbours:
        @pl.when(has(off))
        def _(off=off):
            pl.semaphore_signal(barrier, inc=1, device_id=device(off), device_id_type=MESH)
        count = count + has(off).astype(jnp.int32)

    k = lax.broadcasted_iota(jnp.int32, (256, 128), 0)
    c = lax.broadcasted_iota(jnp.int32, (256, 128), 1)
    pick_m[...] = jnp.where(k // 2 == c, 1.0, 0.0).astype(bf16)
    k, j = k[0:128], c[0:128] % 16
    start_w = jnp.where(j < 7, 84 + 2 * j, 16 + 2 * j)
    pick_w[...] = jnp.where((j < 14) & ((k == start_w) | (k == start_w + 1)), 1.0, 0.0).astype(bf16)

    for t in range(2):
        for f in range(2):
            e[f, t, 0:2] = jnp.zeros((2, 32, 128), f32)
            e[f, t, 18:20] = jnp.zeros((2, 32, 128), f32)
            e[f, t, 2:18, 0:4, :] = jnp.zeros((16, 4, 128), f32)
            e[f, t, 2:18, 20:32, :] = jnp.zeros((16, 12, 128), f32)

    for load in loads:
        load.wait()
    for i, z in ((0, 14), (1, 0)):
        zs[i, 0] = f_v[z : z + 2].astype(f32)
        zs[i, 1] = w_v[z : z + 2]
        ys[i, 0] = f_v[:, z : z + 2, :].astype(f32)
        ys[i, 1] = w_v[:, z : z + 2, :]
    for i, (dz, dy) in enumerate(DIRS[4:]):
        z, y = (15 if dz > 0 else 0), (15 if dy > 0 else 0)
        ds[i, 0:1] = f_v[z, y : y + 1, :].astype(f32)
        ds[i, 1:2] = w_v[z, y : y + 1, :]
    for t in range(2):
        e[0, t, 2:18, 4:20, :] = f_v[:, :, 128 * t : 128 * t + 128].astype(f32)
        e[1, t, 2:18, 4:20, :] = w_v[:, :, 128 * t : 128 * t + 128]

    pl.semaphore_wait(barrier, count)

    def copy(source, target, slot, off):
        return pltpu.make_async_remote_copy(
            src_ref=source, dst_ref=target, send_sem=send_sem.at[slot], recv_sem=recv_sem.at[slot],
            device_id=device(off), device_id_type=MESH)

    def start(messages):
        for source, target, slot, off, fill in messages:
            @pl.when(has(off))
            def _(source=source, target=target, slot=slot, off=off):
                copy(source, target, slot, off).start()

    def receive(messages):
        for source, target, slot, off, fill in messages:
            there = has(negative(off))

            @pl.when(there)
            def _(source=source, target=target, slot=slot, off=off):
                copy(source, target, slot, off).wait_recv()

            @pl.when(jnp.logical_not(there))
            def _(target=target, fill=fill):
                fill(target)

    def sent(messages):
        for source, target, slot, off, fill in messages:
            @pl.when(has(off))
            def _(source=source, target=target, slot=slot, off=off):
                copy(source, target, slot, off).wait_send()

    def fill_pair(target):
        shape = target.shape[1:]
        target[0] = jnp.full(shape, OUTSIDE, f32)
        target[1] = jnp.zeros(shape, f32)

    def fill_row(target):
        row = lax.broadcasted_iota(jnp.int32, (2, 256), 0)
        target[...] = jnp.where(row == 0, OUTSIDE, 0.0).astype(f32)

    def fill_coarse(target):
        shape = target.shape[1:]
        target[0] = jnp.zeros(shape, f32)
        target[1] = jnp.full(shape, OUTSIDE, f32)

    raw = []
    for slot, d in enumerate(DIRS):
        off = d + (0,)
        if slot < 2:
            raw.append((zs.at[slot], zr.at[slot], slot, off, fill_pair))
        elif slot < 4:
            raw.append((ys.at[slot - 2], yr.at[slot - 2], slot, off, fill_pair))
        else:
            raw.append((ds.at[slot - 4], dr.at[slot - 4], slot, off, fill_row))
    start(raw)

    on_top = jnp.where(me["slab"] == size["slab"] - 1, spot_power, 0.0).astype(f32)
    y0, x0 = me["grp"] * 16 - 4, me["brick"] * 256

    def laser(substep, t, r, n):
        lane = lane_of(n)
        y = lax.broadcasted_iota(jnp.int32, (n, 128), 0) + (y0 + r)
        x = x0 + (jnp.where(lane < 64, lane + 224, lane - 96) if t == 2 else lane + 128 * t)
        total = jnp.zeros((n, 128), f32)
        for p in range(4):
            hit = (y == by_ref[substep, p]) & (x == bx_ref[substep, p])
            total = total + jnp.where(hit, on_top, 0.0)
        return total

    receive(raw)
    for t in range(2):
        cols = slice(128 * t, 128 * t + 128)
        for f in range(2):
            e[f, t, 0:2, 4:20, :] = zr[0, f, :, :, cols]
            e[f, t, 18:20, 4:20, :] = zr[1, f, :, :, cols]
            e[f, t, 2:18, 2:4, :] = yr[0, f, :, :, cols]
            e[f, t, 2:18, 20:22, :] = yr[1, f, :, :, cols]
            for i, (dz, dy) in enumerate(DIRS[4:]):
                z, y = (1 if dz > 0 else 18), (3 if dy > 0 else 20)
                e[f, t, z, y : y + 1, :] = dr[i, f : f + 1, cols]

    lane = lane_of(8)
    group = lane // 16
    for f in range(2):
        for v in range(8):
            right, left = jnp.zeros((8, 128), f32), jnp.zeros((8, 128), f32)
            for j in range(8):
                r = 8 * v + j
                if r < 60:
                    z, y = r // 3, 8 * (r % 3)
                    a, b = e[f, 1, z, y : y + 8, :], e[f, 0, z, y : y + 8, :]
                    right = jnp.where(group == j, pltpu.roll(a, (16 * j - 112) % 128, 1), right)
                    left = jnp.where(group == j, pltpu.roll(b, 16 * j, 1) if j else b, left)
            xs[0, f, v] = right
            xs[1, f, v] = left
    along = [(xs.at[i], xr.at[i], 8 + i, (0, 0, 1 - 2 * i), fill_pair) for i in range(2)]
    start(along)

    def raw_t(t, z, r, n):
        return e[1, t, z, r : r + n, :]

    def mid_t(t, z, r, n):
        return t1[t, z, r : r + n, :]

    def put_1(t, z, value):
        t1[t, z, 3:27, :] = value

    def put_2(t, z, value):
        t2[t, z - 2] = value

    def substeps(tiles):
        conductances(e, g, tiles)
        for_24 = functools.partial(raw_t, n=24)
        for_16 = functools.partial(mid_t, n=16)
        thermal(for_24, put_1, g, [laser(0, t, 3, 24) for t in tiles], tiles, 1, 19, 3, 24)
        thermal(for_16, put_2, g, [laser(1, t, 4, 16) for t in tiles], tiles, 2, 18, 4, 16)

    def coarsen(tiles, pick):
        for z in range(8):
            for t in tiles:
                fa, fb = e[0, t, 2 * z + 2, 4:20, :], e[0, t, 2 * z + 3, 4:20, :]
                qs[0, t, z] = fa * t2[t, 2 * z] + fb * t2[t, 2 * z + 1]
                qs[1, t, z] = fa + fb
        rows = []
        for f in range(2):
            pairs = [qs[f, t, :, pl.ds(0, 8, stride=2), :] + qs[f, t, :, pl.ds(1, 8, stride=2), :] for t in tiles]
            pairs = [p.reshape(64, 128) for p in pairs]
            rows.append((jnp.concatenate(pairs, axis=1) if len(pairs) > 1 else pairs[0]) * 0.125)
        q, solid = rows
        q1 = q.astype(bf16)
        rest = q - q1.astype(f32)
        q2 = rest.astype(bf16)
        q3 = (rest - q2.astype(f32)).astype(bf16)
        lhs = jnp.concatenate([q1, q2, q3, solid.astype(bf16)], axis=0)
        out = jnp.dot(lhs, pick[...], preferred_element_type=f32)
        return (out[0:64] + out[64:128]) + out[128:192], out[192:256]

    substeps((0, 1))
    for f, field in enumerate(coarsen((0, 1), pick_m)):
        cbm[f] = field.reshape(8, 8, 128)
    last6, first6 = cbm.at[:, 2:8], cbm.at[:, 0:6]
    swap = []
    for slot, d in enumerate(DIRS):
        off = d + (0,)
        if slot < 2:
            source, target = (last6, first6)[slot], czr.at[slot]
        elif slot < 4:
            source, target = cbm, cyr.at[slot - 2]
        else:
            source, target = (last6 if d[0] > 0 else first6), cdr.at[slot - 4]
        swap.append((source, target, 10 + slot, off, fill_coarse))
    start(swap)

    for f in range(2):
        for r in range(60):
            z, y = r // 3, 8 * (r % 3)
            a, b = e[f, 1, z, y : y + 8, :], e[f, 0, z, y : y + 8, :]
            e[f, 2, z, y : y + 8, :] = jnp.where(lane < 64, pltpu.roll(a, 32, 1), pltpu.roll(b, 96, 1))
        e[f, 2, :, 24:32, :] = jnp.zeros((20, 8, 128), f32)
    receive(along)
    for f in range(2):
        for r in range(60):
            v, j = r // 8, r % 8
            z, y = r // 3, 8 * (r % 3)
            before, after = xr[0, f, v], xr[1, f, v]
            before = pltpu.roll(before, (80 - 16 * j) % 128, 1) if (80 - 16 * j) % 128 else before
            after = pltpu.roll(after, (32 - 16 * j) % 128, 1) if (32 - 16 * j) % 128 else after
            own = jnp.where((lane >= 32) & (lane < 48), after, e[f, 2, z, y : y + 8, :])
            e[f, 2, z, y : y + 8, :] = jnp.where((lane >= 80) & (lane < 96), before, own)

    substeps((2,))
    for f, field in enumerate(coarsen((2,), pick_w)):
        field = field.reshape(8, 8, 128)
        packed = field[0]
        for z in range(1, 8):
            packed = jnp.where(group == z, field[z], packed)
        cbw[f] = packed
    swap_w = [(cbw, cwr.at[slot], 18 + slot, d + (0,), fill_coarse) for slot, d in enumerate(DIRS)]
    start(swap_w)

    lane16 = lane_of(16)
    for z in range(16):
        w = t2[2, z]
        t_v[z, :, 0:128] = jnp.where(lane16 < 16, pltpu.roll(w, 32, 1), t2[0, z])
        t_v[z, :, 128:256] = jnp.where(lane16 >= 112, pltpu.roll(w, 96, 1), t2[1, z])
    saves = [pltpu.make_async_copy(t_v, t_out, out_sem.at[0]), pltpu.make_async_copy(u_v, u_out, out_sem.at[1])]
    saves[0].start()

    def place(main, packed, first, planes, tile):
        for f in range(2):
            p = packed[f]
            for i, z in enumerate(planes):
                rows = slice(8 * tile, 8 * tile + 8)
                left, right = (122 - 16 * z) % 128, (120 - 16 * z) % 128
                a = pltpu.roll(p, left, 1) if left else p
                b = pltpu.roll(p, right, 1) if right else p
                cx[f, 0, first + i, rows, :] = jnp.where(lane == 0, a, jnp.where(lane == 127, b, main[f, i]))
                cx[f, 1, first + i, rows, :] = jnp.where(lane < 6, b, jnp.where(lane >= 122, a, 0.0))

    upper, lower = range(2, 8), range(0, 6)
    place(cbm, cbw, 6, range(8), 1)
    receive(swap)
    receive(swap_w)
    place(czr.at[0], cwr.at[0], 0, upper, 1)
    place(czr.at[1], cwr.at[1], 14, lower, 1)
    place(cyr.at[0], cwr.at[2], 6, range(8), 0)
    place(cyr.at[1], cwr.at[3], 6, range(8), 2)
    for i, (dz, dy) in enumerate(DIRS[4:]):
        place(cdr.at[i], cwr.at[4 + i], 0 if dz > 0 else 14, upper if dz > 0 else lower, 0 if dy > 0 else 2)

    sweeps(cx, u_v, dira, dirb, res, inv, spr, div)
    saves[1].start()
    for save in saves:
        save.wait()
    for messages in (raw, along, swap, swap_w):
        sent(messages)


def sweeps(cx, u, dira, dirb, res, inv, spr, div):
    centre_value = (eigen_high + eigen_low) / 2.0
    radius = (eigen_high - eigen_low) / 2.0
    sigma = centre_value / radius
    rho = 1.0 / sigma
    half = 0.5 * stress_factor
    both = (0, 1)

    for z in range(1, 19):
        s = [cx[0, t, z, 3:27, :] for t in both]
        ahead, behind = next_x(s), prev_x(s)
        for t in both:
            solid = cx[1, t, z, 3:27, :]
            spring = 0.5 + 1.5 * solid
            inverse = jnp.where(solid < -1.0, 0.0, 1.0 / (6.0 * shear_modulus + 2.0 * coupling + spring))
            inv[t, z, 3:27, :] = inverse
            spr[t, z, 3:27, :] = spring + 6.0 * shear_modulus
            scaled = inverse * (1.0 / centre_value)
            force = (
                half * (cx[0, t, z - 1, 3:27, :] - cx[0, t, z + 1, 3:27, :]),
                half * (cx[0, t, z, 2:26, :] - cx[0, t, z, 4:28, :]),
                half * (behind[t] - ahead[t]),
            )
            for d in range(3):
                res[d, t, z, 3:27, :] = force[d]
                dira[d, t, z, 3:27, :] = force[d] * scaled
    for d in range(3):
        u[d] = dira[d, 0, 6:14, 8:16, :]

    old, new = dira, dirb
    for sweep in range(SWEEPS - 1):
        halo = SWEEPS - 2 - sweep
        rho_next = 1.0 / (2.0 * sigma - rho)
        keep, gain = rho_next * rho, 2.0 * rho_next / radius
        first, last, r, n = 6 - halo, 14 + halo, 8 - halo, (16 if halo else 8)
        rows, m = slice(r, r + n), (24 if halo == 4 else 16)
        near = slice(r - 1, r - 1 + m)

        def spread(z):
            x = [old[2, t, z, near, :] for t in both]
            ahead = next_x(x)
            for t in both:
                dz = old[0, t, z + 1, near, :] - old[0, t, z, near, :]
                dy = old[1, t, z, r : r + m, :] - old[1, t, z, near, :]
                div[t, z, near, :] = dz + dy + (ahead[t] - x[t])

        spread(first - 1)
        for z in range(first, last):
            spread(z)
            here = [div[t, z, rows, :] for t in both]
            behind = prev_x(here)
            v = [[old[d, t, z, rows, :] for t in both] for d in range(3)]
            ahead_v, behind_v = [next_x(a) for a in v], [prev_x(a) for a in v]
            for t in both if halo else (0,):
                back = (
                    div[t, z - 1, rows, :] - here[t],
                    div[t, z, r - 1 : r + n - 1, :] - here[t],
                    behind[t] - here[t],
                )
                factor, inverse = spr[t, z, rows, :], inv[t, z, rows, :] * gain
                for d in range(3):
                    side = old[d, t, z, r + 1 : r + n + 1, :] + old[d, t, z, r - 1 : r + n - 1, :]
                    over = old[d, t, z + 1, rows, :] + old[d, t, z - 1, rows, :]
                    around = (ahead_v[d][t] + behind_v[d][t]) + side + over
                    left = res[d, t, z, rows, :] - (factor * v[d][t] - shear_modulus * around + coupling * back[d])
                    ahead_d = keep * v[d][t] + inverse * left
                    if halo:
                        res[d, t, z, rows, :] = left
                        new[d, t, z, rows, :] = ahead_d
                    if t == 0 and 6 <= z < 14:
                        u[d, z - 6] = u[d, z - 6] + ahead_d[8 - r : 16 - r]
        rho = rho_next
        old, new = new, old


def per_device(warmth, flag, north, east):
    vmem = pltpu.VMEM
    ext = lambda *s: vmem(s, f32)
    scratch = [
        ext(16, 16, 256), vmem((16, 16, 256), jnp.int32), pltpu.SMEM((2, 4), jnp.int32), pltpu.SMEM((2, 4), jnp.int32),
        ext(2, 3, 20, 32, 128), ext(4, 3, 20, 32, 128), ext(3, 20, 32, 128), ext(3, 16, 16, 128),
        ext(2, 2, 2, 16, 256), ext(2, 2, 2, 16, 256), ext(2, 2, 16, 2, 256), ext(2, 2, 16, 2, 256), ext(4, 2, 256), ext(4, 2, 256),
        ext(2, 2, 8, 8, 128), ext(2, 2, 8, 8, 128), ext(2, 3, 8, 16, 128),
        ext(2, 8, 8, 128), ext(2, 8, 128), ext(2, 2, 6, 8, 128), ext(2, 2, 8, 8, 128), ext(4, 2, 6, 8, 128), ext(8, 2, 8, 128),
        ext(2, 2, 20, 32, 128), ext(3, 2, 20, 32, 128), ext(3, 2, 20, 32, 128), ext(3, 2, 20, 32, 128),
        ext(2, 20, 32, 128), ext(2, 20, 32, 128), ext(2, 20, 32, 128),
        vmem((256, 128), bf16), vmem((128, 128), bf16), ext(16, 16, 256), ext(3, 8, 8, 128),
        pltpu.SemaphoreType.DMA((4,)), pltpu.SemaphoreType.DMA((26,)), pltpu.SemaphoreType.DMA((26,)), pltpu.SemaphoreType.DMA((2,)),
    ]
    anywhere = pl.BlockSpec(memory_space=pl.ANY)
    return pl.pallas_call(
        kernel,
        out_shape=(jax.ShapeDtypeStruct((16, 16, 256), f32), jax.ShapeDtypeStruct((3, 8, 8, 128), f32)),
        in_specs=[anywhere] * 4,
        out_specs=(anywhere, anywhere),
        scratch_shapes=scratch,
        compiler_params=pltpu.CompilerParams(collective_id=0, has_side_effects=True),
    )(warmth, flag, north, east)


def solution(mesh):
    in_specs = (P("slab", "grp", "brick"), P("slab", "grp", "brick"), P(), P())
    out_specs = (P("slab", "grp", "brick"), P(None, "slab", "grp", "brick"))
    return jax.shard_map(per_device, mesh=mesh, in_specs=in_specs, out_specs=out_specs, check_vma=False)
```

```python
import functools

import jax
import jax.numpy as jnp
from jax import lax
from jax.experimental import pallas as pl
from jax.experimental.pallas import tpu as pltpu
from jax.sharding import PartitionSpec as P

SWEEPS = 6
time_step = 0.15
spot_power = 30.0
shear_modulus = 1.0
coupling = 1.5
stress_factor = 8.0
eigen_low = 0.5
eigen_high = 3.5

MESH = pl.DeviceIdType.MESH
OUTSIDE = -4.0

DIRS = [(1, 0), (-1, 0), (0, 1), (0, -1), (1, 1), (1, -1), (-1, 1), (-1, -1)]

f32 = jnp.float32
bf16 = jnp.bfloat16


def lane_of(rows):
    return lax.broadcasted_iota(jnp.int32, (rows, 128), 1)


def next_x(tiles):
    rolled = [pltpu.roll(t, 127, 1) for t in tiles]
    if len(tiles) == 1:
        return rolled
    end = lane_of(tiles[0].shape[0]) == 127
    return [jnp.where(end, rolled[1 - i], rolled[i]) for i in range(2)]


def prev_x(tiles):
    rolled = [pltpu.roll(t, 1, 1) for t in tiles]
    if len(tiles) == 1:
        return rolled
    end = lane_of(tiles[0].shape[0]) == 0
    return [jnp.where(end, rolled[1 - i], rolled[i]) for i in range(2)]


def conductance(s):
    return jnp.maximum(jnp.maximum(s * (2.0 / 15.0) + 0.2, s * (2.0 / 3.0) - (1.0 / 3.0)), 0.0)


def conductances(e, g, tiles):
    for z in range(19):
        f = [e[0, t, z, 2:26, :] for t in tiles]
        fx = next_x(f) if z else None
        for i, t in enumerate(tiles):
            g[2, t, z, 2:26, :] = conductance(f[i] + e[0, t, z + 1, 2:26, :])
            if z:
                g[0, t, z, 2:26, :] = conductance(f[i] + fx[i])
                g[1, t, z, 2:26, :] = conductance(f[i] + e[0, t, z, 3:27, :])
                g[3, t, z, 2:26, :] = (2.0 * time_step) - time_step * f[i]


def thermal(t_in, t_out, g, source, tiles, first, last, r, n):
    below = [g[2, t, first - 1, r : r + n, :] * (t_in(t, first, r) - t_in(t, first - 1, r)) for t in tiles]
    for z in range(first, last):
        here = [t_in(t, z, r) for t in tiles]
        ahead = next_x(here)
        fx = [g[0, t, z, r : r + n, :] * (ahead[i] - here[i]) for i, t in enumerate(tiles)]
        back = prev_x(fx)
        for i, t in enumerate(tiles):
            fy = g[1, t, z, r : r + n, :] * (t_in(t, z, r + 1) - here[i])
            by = g[1, t, z, r - 1 : r + n - 1, :] * (here[i] - t_in(t, z, r - 1))
            fz = g[2, t, z, r : r + n, :] * (t_in(t, z + 1, r) - here[i])
            total = (fx[i] - back[i]) + (fy - by) + (fz - below[i])
            if z == 17:
                total = total + source[i]
            t_out(t, z, here[i] + g[3, t, z, r : r + n, :] * total)
            below[i] = fz


def kernel(w_hbm, f_hbm, by_hbm, bx_hbm, t_v, u_v,
           w_v, f_v, by_ref, bx_ref, e, g, t1, t2,
           zs, zr, ys, yr, ds, dr, xs, xr, qs, cbm, cbw, czr, cyr, cdr, cwr,
           cx, dira, dirb, res, inv, spr, div, pick_m, pick_w,
           load_sem, send_sem, recv_sem):
    me = {a: lax.axis_index(a) for a in ("slab", "grp", "brick")}
    size = {a: lax.axis_size(a) for a in ("slab", "grp", "brick")}

    def has(off):
        found = None
        for a, d in zip(("slab", "grp", "brick"), off):
            if d:
                one = me[a] < size[a] - 1 if d > 0 else me[a] > 0
                found = one if found is None else found & one
        return found

    def device(off):
        return {a: me[a] + d for a, d in zip(("slab", "grp", "brick"), off)}

    def negative(off):
        return tuple(-d for d in off)

    loads = [
        pltpu.make_async_copy(source, target, load_sem.at[i])
        for i, (source, target) in enumerate(((f_hbm, f_v), (w_hbm, w_v), (by_hbm, by_ref), (bx_hbm, bx_ref)))
    ]
    for load in loads:
        load.start()

    neighbours = [d + (0,) for d in DIRS] + [(0, 0, 1), (0, 0, -1)]
    barrier = pltpu.get_barrier_semaphore()
    count = jnp.int32(0)
    for off in neighbours:
        @pl.when(has(off))
        def _(off=off):
            pl.semaphore_signal(barrier, inc=1, device_id=device(off), device_id_type=MESH)
        count = count + has(off).astype(jnp.int32)

    k = lax.broadcasted_iota(jnp.int32, (256, 128), 0)
    c = lax.broadcasted_iota(jnp.int32, (256, 128), 1)
    pick_m[...] = jnp.where(k // 2 == c, 1.0, 0.0).astype(bf16)
    k, j = k[0:128], c[0:128] % 16
    start_w = jnp.where(j < 7, 84 + 2 * j, 16 + 2 * j)
    pick_w[...] = jnp.where((j < 14) & ((k == start_w) | (k == start_w + 1)), 1.0, 0.0).astype(bf16)

    for t in range(2):
        for f in range(2):
            e[f, t, 0:2] = jnp.zeros((2, 32, 128), f32)
            e[f, t, 18:20] = jnp.zeros((2, 32, 128), f32)
            e[f, t, 2:18, 0:4, :] = jnp.zeros((16, 4, 128), f32)
            e[f, t, 2:18, 20:32, :] = jnp.zeros((16, 12, 128), f32)

    for load in loads:
        load.wait()
    for i, z in ((0, 14), (1, 0)):
        zs[i, 0] = f_v[z : z + 2].astype(f32)
        zs[i, 1] = w_v[z : z + 2]
        ys[i, 0] = f_v[:, z : z + 2, :].astype(f32)
        ys[i, 1] = w_v[:, z : z + 2, :]
    for i, (dz, dy) in enumerate(DIRS[4:]):
        z, y = (15 if dz > 0 else 0), (15 if dy > 0 else 0)
        ds[i, 0:1] = f_v[z, y : y + 1, :].astype(f32)
        ds[i, 1:2] = w_v[z, y : y + 1, :]
    for t in range(2):
        e[0, t, 2:18, 4:20, :] = f_v[:, :, 128 * t : 128 * t + 128].astype(f32)
        e[1, t, 2:18, 4:20, :] = w_v[:, :, 128 * t : 128 * t + 128]

    pl.semaphore_wait(barrier, count)

    def copy(source, target, slot, off):
        return pltpu.make_async_remote_copy(
            src_ref=source, dst_ref=target, send_sem=send_sem.at[slot], recv_sem=recv_sem.at[slot],
            device_id=device(off), device_id_type=MESH)

    def start(messages):
        for source, target, slot, off, fill in messages:
            @pl.when(has(off))
            def _(source=source, target=target, slot=slot, off=off):
                copy(source, target, slot, off).start()

    def receive(messages):
        for source, target, slot, off, fill in messages:
            there = has(negative(off))

            @pl.when(there)
            def _(source=source, target=target, slot=slot, off=off):
                copy(source, target, slot, off).wait_recv()

            @pl.when(jnp.logical_not(there))
            def _(target=target, fill=fill):
                fill(target)

    def sent(messages):
        for source, target, slot, off, fill in messages:
            @pl.when(has(off))
            def _(source=source, target=target, slot=slot, off=off):
                copy(source, target, slot, off).wait_send()

    def fill_pair(target):
        shape = target.shape[1:]
        target[0] = jnp.full(shape, OUTSIDE, f32)
        target[1] = jnp.zeros(shape, f32)

    def fill_row(target):
        row = lax.broadcasted_iota(jnp.int32, (2, 256), 0)
        target[...] = jnp.where(row == 0, OUTSIDE, 0.0).astype(f32)

    def fill_coarse(target):
        shape = target.shape[1:]
        target[0] = jnp.zeros(shape, f32)
        target[1] = jnp.full(shape, OUTSIDE, f32)

    raw = []
    for slot, d in enumerate(DIRS):
        off = d + (0,)
        if slot < 2:
            raw.append((zs.at[slot], zr.at[slot], slot, off, fill_pair))
        elif slot < 4:
            raw.append((ys.at[slot - 2], yr.at[slot - 2], slot, off, fill_pair))
        else:
            raw.append((ds.at[slot - 4], dr.at[slot - 4], slot, off, fill_row))
    start(raw)

    on_top = jnp.where(me["slab"] == size["slab"] - 1, spot_power, 0.0).astype(f32)
    y0, x0 = me["grp"] * 16 - 4, me["brick"] * 256

    def laser(substep, t, r, n):
        lane = lane_of(n)
        y = lax.broadcasted_iota(jnp.int32, (n, 128), 0) + (y0 + r)
        x = x0 + (jnp.where(lane < 64, lane + 224, lane - 96) if t == 2 else lane + 128 * t)
        total = jnp.zeros((n, 128), f32)
        for p in range(4):
            hit = (y == by_ref[substep, p]) & (x == bx_ref[substep, p])
            total = total + jnp.where(hit, on_top, 0.0)
        return total

    receive(raw)
    for t in range(2):
        cols = slice(128 * t, 128 * t + 128)
        for f in range(2):
            e[f, t, 0:2, 4:20, :] = zr[0, f, :, :, cols]
            e[f, t, 18:20, 4:20, :] = zr[1, f, :, :, cols]
            e[f, t, 2:18, 2:4, :] = yr[0, f, :, :, cols]
            e[f, t, 2:18, 20:22, :] = yr[1, f, :, :, cols]
            for i, (dz, dy) in enumerate(DIRS[4:]):
                z, y = (1 if dz > 0 else 18), (3 if dy > 0 else 20)
                e[f, t, z, y : y + 1, :] = dr[i, f : f + 1, cols]

    lane = lane_of(8)
    group = lane // 16
    for f in range(2):
        for v in range(8):
            right, left = jnp.zeros((8, 128), f32), jnp.zeros((8, 128), f32)
            for j in range(8):
                r = 8 * v + j
                if r < 60:
                    z, y = r // 3, 8 * (r % 3)
                    a, b = e[f, 1, z, y : y + 8, :], e[f, 0, z, y : y + 8, :]
                    right = jnp.where(group == j, pltpu.roll(a, (16 * j - 112) % 128, 1), right)
                    left = jnp.where(group == j, pltpu.roll(b, 16 * j, 1) if j else b, left)
            xs[0, f, v] = right
            xs[1, f, v] = left
    along = [(xs.at[i], xr.at[i], 8 + i, (0, 0, 1 - 2 * i), fill_pair) for i in range(2)]
    start(along)

    def raw_t(t, z, r, n):
        return e[1, t, z, r : r + n, :]

    def mid_t(t, z, r, n):
        return t1[t, z, r : r + n, :]

    def put_1(t, z, value):
        t1[t, z, 3:27, :] = value

    def put_2(t, z, value):
        t2[t, z - 2] = value

    def substeps(tiles):
        conductances(e, g, tiles)
        for_24 = functools.partial(raw_t, n=24)
        for_16 = functools.partial(mid_t, n=16)
        thermal(for_24, put_1, g, [laser(0, t, 3, 24) for t in tiles], tiles, 1, 19, 3, 24)
        thermal(for_16, put_2, g, [laser(1, t, 4, 16) for t in tiles], tiles, 2, 18, 4, 16)

    def coarsen(tiles, pick):
        for z in range(8):
            for t in tiles:
                fa, fb = e[0, t, 2 * z + 2, 4:20, :], e[0, t, 2 * z + 3, 4:20, :]
                qs[0, t, z] = fa * t2[t, 2 * z] + fb * t2[t, 2 * z + 1]
                qs[1, t, z] = fa + fb
        rows = []
        for f in range(2):
            pairs = [qs[f, t, :, pl.ds(0, 8, stride=2), :] + qs[f, t, :, pl.ds(1, 8, stride=2), :] for t in tiles]
            pairs = [p.reshape(64, 128) for p in pairs]
            rows.append((jnp.concatenate(pairs, axis=1) if len(pairs) > 1 else pairs[0]) * 0.125)
        q, solid = rows
        q1 = q.astype(bf16)
        rest = q - q1.astype(f32)
        q2 = rest.astype(bf16)
        q3 = (rest - q2.astype(f32)).astype(bf16)
        lhs = jnp.concatenate([q1, q2, q3, solid.astype(bf16)], axis=0)
        out = jnp.dot(lhs, pick[...], preferred_element_type=f32)
        return (out[0:64] + out[64:128]) + out[128:192], out[192:256]

    substeps((0, 1))
    for f, field in enumerate(coarsen((0, 1), pick_m)):
        cbm[f] = field.reshape(8, 8, 128)
    last6, first6 = cbm.at[:, 2:8], cbm.at[:, 0:6]
    swap = []
    for slot, d in enumerate(DIRS):
        off = d + (0,)
        if slot < 2:
            source, target = (last6, first6)[slot], czr.at[slot]
        elif slot < 4:
            source, target = cbm, cyr.at[slot - 2]
        else:
            source, target = (last6 if d[0] > 0 else first6), cdr.at[slot - 4]
        swap.append((source, target, 10 + slot, off, fill_coarse))
    start(swap)

    for f in range(2):
        for r in range(60):
            z, y = r // 3, 8 * (r % 3)
            a, b = e[f, 1, z, y : y + 8, :], e[f, 0, z, y : y + 8, :]
            e[f, 2, z, y : y + 8, :] = jnp.where(lane < 64, pltpu.roll(a, 32, 1), pltpu.roll(b, 96, 1))
        e[f, 2, :, 24:32, :] = jnp.zeros((20, 8, 128), f32)
    receive(along)
    for f in range(2):
        for r in range(60):
            v, j = r // 8, r % 8
            z, y = r // 3, 8 * (r % 3)
            before, after = xr[0, f, v], xr[1, f, v]
            before = pltpu.roll(before, (80 - 16 * j) % 128, 1) if (80 - 16 * j) % 128 else before
            after = pltpu.roll(after, (32 - 16 * j) % 128, 1) if (32 - 16 * j) % 128 else after
            own = jnp.where((lane >= 32) & (lane < 48), after, e[f, 2, z, y : y + 8, :])
            e[f, 2, z, y : y + 8, :] = jnp.where((lane >= 80) & (lane < 96), before, own)

    substeps((2,))
    for f, field in enumerate(coarsen((2,), pick_w)):
        field = field.reshape(8, 8, 128)
        packed = field[0]
        for z in range(1, 8):
            packed = jnp.where(group == z, field[z], packed)
        cbw[f] = packed
    swap_w = [(cbw, cwr.at[slot], 18 + slot, d + (0,), fill_coarse) for slot, d in enumerate(DIRS)]
    start(swap_w)

    lane16 = lane_of(16)
    for z in range(16):
        w = t2[2, z]
        t_v[z, :, 0:128] = jnp.where(lane16 < 16, pltpu.roll(w, 32, 1), t2[0, z])
        t_v[z, :, 128:256] = jnp.where(lane16 >= 112, pltpu.roll(w, 96, 1), t2[1, z])

    def place(main, packed, first, planes, tile):
        for f in range(2):
            p = packed[f]
            for i, z in enumerate(planes):
                rows = slice(8 * tile, 8 * tile + 8)
                left, right = (122 - 16 * z) % 128, (120 - 16 * z) % 128
                a = pltpu.roll(p, left, 1) if left else p
                b = pltpu.roll(p, right, 1) if right else p
                cx[f, 0, first + i, rows, :] = jnp.where(lane == 0, a, jnp.where(lane == 127, b, main[f, i]))
                cx[f, 1, first + i, rows, :] = jnp.where(lane < 6, b, jnp.where(lane >= 122, a, 0.0))

    upper, lower = range(2, 8), range(0, 6)
    place(cbm, cbw, 6, range(8), 1)
    receive(swap)
    receive(swap_w)
    place(czr.at[0], cwr.at[0], 0, upper, 1)
    place(czr.at[1], cwr.at[1], 14, lower, 1)
    place(cyr.at[0], cwr.at[2], 6, range(8), 0)
    place(cyr.at[1], cwr.at[3], 6, range(8), 2)
    for i, (dz, dy) in enumerate(DIRS[4:]):
        place(cdr.at[i], cwr.at[4 + i], 0 if dz > 0 else 14, upper if dz > 0 else lower, 0 if dy > 0 else 2)

    sweeps(cx, u_v, dira, dirb, res, inv, spr, div)
    for messages in (raw, along, swap, swap_w):
        sent(messages)


def sweeps(cx, u, dira, dirb, res, inv, spr, div):
    centre_value = (eigen_high + eigen_low) / 2.0
    radius = (eigen_high - eigen_low) / 2.0
    sigma = centre_value / radius
    rho = 1.0 / sigma
    half = 0.5 * stress_factor
    both = (0, 1)

    for z in range(1, 19):
        s = [cx[0, t, z, 3:27, :] for t in both]
        ahead, behind = next_x(s), prev_x(s)
        for t in both:
            solid = cx[1, t, z, 3:27, :]
            spring = 0.5 + 1.5 * solid
            inverse = jnp.where(solid < -1.0, 0.0, 1.0 / (6.0 * shear_modulus + 2.0 * coupling + spring))
            inv[t, z, 3:27, :] = inverse
            spr[t, z, 3:27, :] = spring + 6.0 * shear_modulus
            scaled = inverse * (1.0 / centre_value)
            force = (
                half * (cx[0, t, z - 1, 3:27, :] - cx[0, t, z + 1, 3:27, :]),
                half * (cx[0, t, z, 2:26, :] - cx[0, t, z, 4:28, :]),
                half * (behind[t] - ahead[t]),
            )
            for d in range(3):
                res[d, t, z, 3:27, :] = force[d]
                dira[d, t, z, 3:27, :] = force[d] * scaled
    for d in range(3):
        u[d] = dira[d, 0, 6:14, 8:16, :]

    old, new = dira, dirb
    for sweep in range(SWEEPS - 1):
        halo = SWEEPS - 2 - sweep
        rho_next = 1.0 / (2.0 * sigma - rho)
        keep, gain = rho_next * rho, 2.0 * rho_next / radius
        first, last, r, n = 6 - halo, 14 + halo, 8 - halo, (16 if halo else 8)
        rows, m = slice(r, r + n), (24 if halo == 4 else 16)
        near = slice(r - 1, r - 1 + m)

        def spread(z):
            x = [old[2, t, z, near, :] for t in both]
            ahead = next_x(x)
            for t in both:
                dz = old[0, t, z + 1, near, :] - old[0, t, z, near, :]
                dy = old[1, t, z, r : r + m, :] - old[1, t, z, near, :]
                div[t, z, near, :] = dz + dy + (ahead[t] - x[t])

        spread(first - 1)
        for z in range(first, last):
            spread(z)
            here = [div[t, z, rows, :] for t in both]
            behind = prev_x(here)
            v = [[old[d, t, z, rows, :] for t in both] for d in range(3)]
            ahead_v, behind_v = [next_x(a) for a in v], [prev_x(a) for a in v]
            for t in both if halo else (0,):
                back = (
                    div[t, z - 1, rows, :] - here[t],
                    div[t, z, r - 1 : r + n - 1, :] - here[t],
                    behind[t] - here[t],
                )
                factor, inverse = spr[t, z, rows, :], inv[t, z, rows, :] * gain
                for d in range(3):
                    side = old[d, t, z, r + 1 : r + n + 1, :] + old[d, t, z, r - 1 : r + n - 1, :]
                    over = old[d, t, z + 1, rows, :] + old[d, t, z - 1, rows, :]
                    around = (ahead_v[d][t] + behind_v[d][t]) + side + over
                    left = res[d, t, z, rows, :] - (factor * v[d][t] - shear_modulus * around + coupling * back[d])
                    ahead_d = keep * v[d][t] + inverse * left
                    if halo:
                        res[d, t, z, rows, :] = left
                        new[d, t, z, rows, :] = ahead_d
                    if t == 0 and 6 <= z < 14:
                        u[d, z - 6] = u[d, z - 6] + ahead_d[8 - r : 16 - r]
        rho = rho_next
        old, new = new, old


def per_device(warmth, flag, north, east):
    vmem = pltpu.VMEM
    ext = lambda *s: vmem(s, f32)
    scratch = [
        ext(16, 16, 256), vmem((16, 16, 256), jnp.int32), pltpu.SMEM((2, 4), jnp.int32), pltpu.SMEM((2, 4), jnp.int32),
        ext(2, 3, 20, 32, 128), ext(4, 3, 20, 32, 128), ext(3, 20, 32, 128), ext(3, 16, 16, 128),
        ext(2, 2, 2, 16, 256), ext(2, 2, 2, 16, 256), ext(2, 2, 16, 2, 256), ext(2, 2, 16, 2, 256), ext(4, 2, 256), ext(4, 2, 256),
        ext(2, 2, 8, 8, 128), ext(2, 2, 8, 8, 128), ext(2, 3, 8, 16, 128),
        ext(2, 8, 8, 128), ext(2, 8, 128), ext(2, 2, 6, 8, 128), ext(2, 2, 8, 8, 128), ext(4, 2, 6, 8, 128), ext(8, 2, 8, 128),
        ext(2, 2, 20, 32, 128), ext(3, 2, 20, 32, 128), ext(3, 2, 20, 32, 128), ext(3, 2, 20, 32, 128),
        ext(2, 20, 32, 128), ext(2, 20, 32, 128), ext(2, 20, 32, 128),
        vmem((256, 128), bf16), vmem((128, 128), bf16),
        pltpu.SemaphoreType.DMA((4,)), pltpu.SemaphoreType.DMA((26,)), pltpu.SemaphoreType.DMA((26,)),
    ]
    anywhere = pl.BlockSpec(memory_space=pl.ANY)
    local = pl.BlockSpec(memory_space=pltpu.VMEM)
    shapes = (jax.ShapeDtypeStruct((16, 16, 256), f32), jax.ShapeDtypeStruct((3, 8, 8, 128), f32))
    results = pl.pallas_call(
        kernel,
        out_shape=shapes,
        in_specs=[pl.BlockSpec(memory_space=pltpu.HBM)] * 4,
        out_specs=(local, local),
        scratch_shapes=scratch,
        compiler_params=pltpu.CompilerParams(collective_id=0, has_side_effects=True, vmem_limit_bytes=56098816),
    )(warmth, flag, north, east)
    return pl.pallas_call(
        store,
        out_shape=shapes,
        in_specs=[local, local],
        out_specs=(anywhere, anywhere),
        scratch_shapes=[pltpu.SemaphoreType.DMA((2,))],
        compiler_params=pltpu.CompilerParams(vmem_limit_bytes=4 * 2**20),
    )(*results)


def store(t, u, t_out, u_out, sem):
    copies = [pltpu.make_async_copy(t, t_out, sem.at[0]), pltpu.make_async_copy(u, u_out, sem.at[1])]
    for copy in copies:
        copy.start()
    for copy in copies:
        copy.wait()


def solution(mesh):
    in_specs = (P("slab", "grp", "brick"), P("slab", "grp", "brick"), P(), P())
    out_specs = (P("slab", "grp", "brick"), P(None, "slab", "grp", "brick"))
    return jax.shard_map(per_device, mesh=mesh, in_specs=in_specs, out_specs=out_specs, check_vma=False)
```
